32 devices in a mesh: wide: 8 (over z, y), narrow: 4 (over x, core).
Axes of the slice: x: 2, y: 2, z: 4, core: 2. Of those that a mesh axis runs over, the one named last changes fastest.
Arguments:
- tokens: bfloat16 [4, 16384, 1024], P(None, 'wide', 'narrow'), may hold values from -6 to 6
- cotangent: bfloat16 [4, 16384, 1024], P(None, 'wide', 'narrow'), may hold values from -6 to 6
- lengths: int32 [4, 8], P(None, 'wide'), may hold values from 1024 to 2048, as said below
- routes: int32 [4, 8, 256], P(None, 'wide'), may hold values from 0 to 2047, as said below
- qkv_weight: bfloat16 [1024, 3, 1024], P('wide', None, 'narrow'), may hold values from -0.1875 to 0.1875
- out_weight: bfloat16 [1024, 1024], P('wide', 'narrow'), may hold values from -2 to 2
- up_weight: bfloat16 [1024, 4096], P('wide', 'narrow'), may hold values from -0.1875 to 0.1875
- down_weight: bfloat16 [1024, 4096], P('wide', 'narrow'), may hold values from -0.09375 to 0.09375
- first_gain: bfloat16 [1024], P('wide'), may hold values from 0.5 to 1.5
- first_bias: bfloat16 [1024], P('wide'), may hold values from -2 to 2
- second_gain: bfloat16 [1024], P('wide'), may hold values from 0.5 to 1.5
- second_bias: bfloat16 [1024], P('wide'), may hold values from -2 to 2
- router_weight: bfloat16 [1024], P('wide'), may hold values from -0.1875 to 0.1875
Outputs:
- mixed: bfloat16 [4, 16384, 1024], P(None, 'wide', 'narrow')
- tokens_grad: bfloat16 [4, 16384, 1024], P(None, 'wide', 'narrow')
- qkv_grad: float32 [1024, 3, 1024], P('wide', None, 'narrow')
- out_grad: float32 [1024, 1024], P('wide', 'narrow')
- up_grad: float32 [1024, 4096], P('wide', 'narrow')
- down_grad: float32 [1024, 4096], P('wide', 'narrow')
- first_gain_grad: float32 [1024], P('wide')
- first_bias_grad: float32 [1024], P('wide')
- second_gain_grad: float32 [1024], P('wide')
- second_bias_grad: float32 [1024], P('wide')
- router_grad: float32 [1024], P('wide')
The draws below stay inside these ranges and needn't reach their ends.
Inputs may be any that keep to these rules, and one draw needn't show every extreme that they name: `lengths`: every length is a multiple of 8; in every draw some sequence has exactly 2048 tokens and some other exactly 1024. `routes`: for sequence s of micro-batch m, slots 0 to lengths[m, s] // 8 - 1 hold distinct positions below lengths[m, s] in rising order; the later slots hold positions below 2048 that are not routed.
All inputs are finite; a program needn't handle non-finite values.
Results may differ from the reference program's by a relative error of at most 0.011.
Values may be sent and summed in bfloat16 or wider, within the bound.
No kernel may reach another device: no remote copies, remote signals or barrier semaphores. Data moves between devices by JAX's collectives and lax.ppermute only.
A program may use at most 88 MiB of HBM per device.

```python
import jax
import jax.numpy as jnp
from jax import lax

MODEL_WIDTH = 1024
HEADS = 16
HEAD_DIM = 64
FF = 4096
MB = 4
WIDE_SEQUENCES = 1
LEN = 2048
ROUTED_SLOTS = 256
NSEQ = 8
N_WIDE = 8


def route_plan(key):
    total_seqs = MB * NSEQ
    length_key = jax.random.fold_in(key, 11)
    drawn = 8 * jax.random.randint(length_key, (total_seqs,), LEN // 16, LEN // 8 + 1)
    longest_at = jax.random.randint(jax.random.fold_in(key, 12), (), 0, total_seqs)
    shortest_at = (longest_at + 1 + jax.random.randint(jax.random.fold_in(key, 14), (), 0, total_seqs - 1)) % total_seqs
    seq_ids = jnp.arange(total_seqs)
    drawn = jnp.where(seq_ids == shortest_at, LEN // 2, drawn)
    drawn = jnp.where(seq_ids == longest_at, LEN, drawn).astype(jnp.int32)
    seq_keys = jax.random.split(jax.random.fold_in(key, 13), total_seqs)

    def choose(one_key, length):
        order_rank = jax.random.permutation(one_key, LEN).astype(jnp.int32)
        places = jnp.arange(LEN, dtype=jnp.int32)
        masked = jnp.where(places < length, order_rank, LEN + places)
        ranked = jnp.argsort(masked, stable=True)[:LEN // 8].astype(jnp.int32)
        slot_ids = jnp.arange(LEN // 8, dtype=jnp.int32)
        is_live = slot_ids < length // 8
        lifted = jnp.where(is_live, ranked, LEN + ranked)
        sorted_slots = jnp.sort(lifted)
        return jnp.where(is_live, sorted_slots, sorted_slots - LEN).astype(jnp.int32)
    chosen_slots = jax.vmap(choose)(seq_keys, drawn)
    return (drawn.reshape(MB, NSEQ), chosen_slots.reshape(MB, NSEQ, LEN // 8))


def draw_lengths(key, part):
    return route_plan(key)[0]


def draw_routes(key, part):
    return route_plan(key)[1]


def steps_of(stream_key, shape, shards, low, high):
    factor_of = 1.0
    for position, shards_of in shards:
        heights = jax.random.uniform(jax.random.fold_in(jax.random.fold_in(stream_key, 6), position), (shards_of,), jnp.float32, low / len(shards), high / len(shards))
        factor_of = factor_of * jnp.repeat(jnp.exp(heights), shape[position] // shards_of).reshape((-1,) + (1,) * (len(shape) - 1 - position))
    return factor_of


def bell_draw(key, shape, width, reach, shards=(), kind=jnp.bfloat16):
    values = jax.random.normal(key, shape, jnp.float32) * width
    if len(shards) > 0:
        values = steps_of(key, shape, shards, -0.22, 0.18) * values
    return jnp.clip(values, min=-reach, max=reach).astype(kind)


def setup_inputs(seed: int = 0) -> dict:
    key_of = jax.random.split(jax.random.key(seed), 14)
    return {
        "tokens": bell_draw(key_of[0], (MB, NSEQ * LEN, MODEL_WIDTH), 1.0, 6.0, ((1, 8), (2, 4))),
        "cotangent": bell_draw(key_of[1], (MB, NSEQ * LEN, MODEL_WIDTH), 1.0, 6.0, ((1, 8), (2, 4))),
        "lengths": draw_lengths(jax.random.fold_in(key_of[13], 71), 0),
        "routes": draw_routes(jax.random.fold_in(key_of[13], 71), 0),
        "qkv_weight": bell_draw(key_of[4], (MODEL_WIDTH, 3, MODEL_WIDTH), MODEL_WIDTH ** -0.5, 0.1875, ((0, 8), (2, 4))),
        "out_weight": bell_draw(key_of[5], (MODEL_WIDTH, MODEL_WIDTH), (2 * MODEL_WIDTH // ROUTED_SLOTS) ** -0.5, 2.0, ((0, 8), (1, 4))),
        "up_weight": bell_draw(key_of[6], (MODEL_WIDTH, FF), MODEL_WIDTH ** -0.5, 0.1875, ((0, 8), (1, 4))),
        "down_weight": bell_draw(key_of[7], (MODEL_WIDTH, FF), FF ** -0.5, 0.09375, ((0, 8), (1, 4))),
        "first_gain": jnp.clip(1.0 + 0.1 * jax.random.normal(key_of[8], (MODEL_WIDTH,), jnp.float32), 0.5, 1.5).astype(jnp.bfloat16),
        "first_bias": bell_draw(key_of[9], (MODEL_WIDTH,), 0.3, 2.0, ((0, 8),)),
        "second_gain": jnp.clip(1.0 + 0.1 * jax.random.normal(key_of[10], (MODEL_WIDTH,), jnp.float32), 0.5, 1.5).astype(jnp.bfloat16),
        "second_bias": bell_draw(key_of[11], (MODEL_WIDTH,), 0.3, 2.0, ((0, 8),)),
        "router_weight": bell_draw(key_of[12], (MODEL_WIDTH,), MODEL_WIDTH ** -0.5, 0.1875, ((0, 8),)),
    }


@jax.custom_vjp
def low(v):
    return lax.optimization_barrier(v.astype(jnp.bfloat16)).astype(jnp.float32)

@jax.custom_vjp
def low_back(v):
    return v

def low_keep(v):
    return (low(v), None)

def low_pass(kept, grad):
    return (grad,)

def back_keep(v):
    return (v, None)

def back_low(kept, grad):
    return (low(grad),)
low.defvjp(low_keep, low_pass)
low_back.defvjp(back_keep, back_low)
EPSILON = 1e-05

def layer_norm(values, gain_row, shift_row):
    center = values - lax.optimization_barrier(jnp.mean(values, axis=-1, keepdims=True))
    spread = lax.optimization_barrier(jnp.mean(center * center, axis=-1, keepdims=True))
    return center * lax.rsqrt(spread + EPSILON) * gain_row + shift_row

def group_forward(token_rows_block, weights, route_block, length_block):
    highest_scores = lax.Precision.HIGHEST
    qkv_full, out_full, up_full, down_full, gain_one, bias_one, gain_two, bias_two, router = weights
    positions = jnp.arange(LEN, dtype=jnp.int32)
    is_live = jnp.arange(ROUTED_SLOTS, dtype=jnp.int32)[None, :] < (length_block // 8)[:, None]
    slot_indicator = jnp.where((route_block[:, :, None] == positions[None, None, :]) & is_live[:, :, None], 1.0, 0.0).astype(jnp.float32)
    chosen_tokens = jnp.einsum('emp,epf->emf', slot_indicator, token_rows_block, precision=highest_scores).reshape(WIDE_SEQUENCES * ROUTED_SLOTS, MODEL_WIDTH)
    router_gate = jnp.dot(chosen_tokens, router, precision=highest_scores)
    normed = low(layer_norm(chosen_tokens, gain_one, bias_one))
    qkv = jnp.einsum('rd,dcn->rcn', normed, qkv_full, precision=highest_scores)
    qkv = low(low_back(qkv))
    split_qkv = qkv.reshape(WIDE_SEQUENCES, ROUTED_SLOTS, 3, HEADS, HEAD_DIM)
    query_heads = split_qkv[:, :, 0]
    key_heads = split_qkv[:, :, 1]
    value_heads = split_qkv[:, :, 2]
    score_scale = HEAD_DIM ** (-0.5)
    scores = jnp.einsum('sqhd,skhd->shqk', query_heads, key_heads, precision=highest_scores) * score_scale
    scores = low_back(scores)
    causal = jnp.arange(ROUTED_SLOTS)[:, None] >= jnp.arange(ROUTED_SLOTS)[None, :]
    scores = jnp.where(causal, scores, -1e+30)
    probs_low = low(jax.nn.softmax(scores, axis=-1))
    heads_out = jnp.einsum('shqk,skhd->sqhd', probs_low, value_heads, precision=highest_scores).reshape(WIDE_SEQUENCES * ROUTED_SLOTS, MODEL_WIDTH)
    heads_out = low(low_back(heads_out))
    attended = low_back(jnp.dot(heads_out, out_full.T, precision=highest_scores))
    second = chosen_tokens + attended
    normed_two = low(layer_norm(second, gain_two, bias_two))
    hidden_pre = low_back(jnp.dot(normed_two, up_full, precision=highest_scores))
    activated = low(jax.nn.gelu(hidden_pre, approximate=True))
    expanded = low_back(jnp.dot(activated, down_full.T, precision=highest_scores))
    residual_update = router_gate[:, None] * (attended + expanded)
    return token_rows_block + jnp.einsum('yti,yto->yio', slot_indicator, residual_update.reshape(WIDE_SEQUENCES, ROUTED_SLOTS, MODEL_WIDTH), precision=highest_scores)

def reference(tokens, cotangent, lengths, routes, qkv_weight, out_weight, up_weight, down_weight, first_gain, first_bias, second_gain, second_bias, router_weight):
    weights = tuple((param.astype(jnp.float32) for param in (qkv_weight, out_weight, up_weight, down_weight, first_gain, first_bias, second_gain, second_bias, router_weight)))
    groups = MB * N_WIDE
    token_groups = tokens.astype(jnp.float32).reshape(groups, WIDE_SEQUENCES, LEN, MODEL_WIDTH)
    cot_groups = cotangent.astype(jnp.float32).reshape(groups, WIDE_SEQUENCES, LEN, MODEL_WIDTH)
    length_groups = lengths.reshape(groups, WIDE_SEQUENCES)
    route_groups = routes.reshape(groups, WIDE_SEQUENCES, ROUTED_SLOTS)

    def advance(grad_totals, inputs_now):
        token_rows_block, cot_block, length_block, route_block = inputs_now

        def forward(token_in, weight_in):
            return group_forward(token_in, weight_in, route_block, length_block)
        result, pullback = jax.vjp(forward, token_rows_block, weights)
        token_grad, weight_grad = pullback(cot_block)
        grad_totals = tuple((total + piece for total, piece in zip(grad_totals, weight_grad)))
        return (grad_totals, (result.astype(jnp.bfloat16), token_grad.astype(jnp.bfloat16)))
    start = tuple((jnp.zeros_like(weight) for weight in weights))
    final, (mixed, token_grads) = lax.scan(advance, start, (token_groups, cot_groups, length_groups, route_groups))
    mixed = mixed.reshape(MB, NSEQ * LEN, MODEL_WIDTH)
    token_grads = token_grads.reshape(MB, NSEQ * LEN, MODEL_WIDTH)
    return (mixed, token_grads, final[0], final[1], final[2], final[3], final[4], final[5], final[6], final[7], final[8])
```

```python
import jax
import jax.numpy as jnp
from jax import lax
from jax.sharding import PartitionSpec as P

HEAD_DIM = 64
EPSILON = 1e-05


F32 = jnp.float32
BF16 = jnp.bfloat16


def bit_groups(count):
    bits = count.bit_length() - 1
    groups = []
    low = bits
    while low > 1:
        width = 2 if (low - 1) % 2 == 0 else 1
        groups.append((low - width, width))
        low -= width
    if low == 1:
        groups.append((0, 1))
    return groups


def swap(value, axis, count, mask):
    return lax.ppermute(value, axis, [(i, i ^ mask) for i in range(count)])


def in_order(pieces, digit):
    bit = 1
    while bit < len(pieces):
        flip = (digit & bit) != 0
        pieces = [
            jnp.where(flip, pieces[p ^ bit], pieces[p]) for p in range(len(pieces))
        ]
        bit *= 2
    return pieces


def gather_wide(block, index, count):
    held = block[None]
    for low, width in bit_groups(count):
        group = 1 << width
        digit = (index >> low) & (group - 1)
        pieces = [held] + [swap(held, "wide", count, s << low) for s in range(1, group)]
        held = jnp.stack(in_order(pieces, digit), axis=1)
        held = held.reshape((-1,) + block.shape)
    return held


def scatter_rest(kept, index, count):
    groups = bit_groups(count)[:-1]
    for low, width in reversed(groups):
        group = 1 << width
        digit = (index >> low) & (group - 1)
        parts = kept.reshape((-1, group) + kept.shape[1:])
        take = lambda s: lax.dynamic_index_in_dim(parts, digit ^ s, 1, keepdims=False)
        received = [
            swap(take(s).astype(BF16), "wide", count, s << low) for s in range(1, group)
        ]
        kept = take(0)
        for piece in received:
            kept = kept + piece.astype(F32)
    return kept[0]


def contract_last(left, right):
    return lax.dot_general(left, right, (((1,), (1,)), ((), ())), preferred_element_type=F32)


def contract_first(left, right):
    return lax.dot_general(left, right, (((0,), (0,)), ((), ())), preferred_element_type=F32)


def weight_grad(left, right, index, count):
    depth = left.shape[1]
    block = depth // count
    split = left.reshape(left.shape[0], count // 2, 2, block)
    low = index & 1
    pick = lambda which: lax.dynamic_index_in_dim(split, which, 2, keepdims=False).reshape(
        left.shape[0], depth // 2
    )
    sent = contract_first(pick(1 - low), right).astype(BF16)
    received = swap(sent, "wide", count, 1)
    kept = contract_first(pick(low), right) + received.astype(F32)
    return scatter_rest(kept.reshape(count // 2, block, -1), index, count)


def gather_narrow(own, lane_x, lane_core):
    across = swap(own, "narrow", 4, 2)
    beside = swap(own, "narrow", 4, 1)
    diagonal = swap(across, "narrow", 4, 1)
    first = in_order([own, beside], lane_core)
    second = in_order([across, diagonal], lane_core)
    near = jnp.concatenate(first, axis=-1)
    far = jnp.concatenate(second, axis=-1)
    return jnp.concatenate(in_order([near, far], lane_x), axis=-1)


def sum_narrow(part, lane_core):
    half = part.shape[1] // 2
    sent = lax.dynamic_slice_in_dim(part, (1 - lane_core) * half, half, 1).astype(BF16)
    kept = lax.dynamic_slice_in_dim(part, lane_core * half, half, 1)
    chip = (kept + swap(sent, "narrow", 4, 1).astype(F32)).astype(BF16)
    total = (chip.astype(F32) + swap(chip, "narrow", 4, 2).astype(F32)).astype(BF16)
    return jnp.concatenate(in_order([total, swap(total, "narrow", 4, 1)], lane_core), axis=1)


def scatter_narrow(part, lane_x, lane_core):
    rows, width = part.shape
    split = part.reshape(rows, 2, 2, width // 4)
    sent = lax.dynamic_index_in_dim(split, 1 - lane_core, 2, keepdims=False).astype(BF16)
    kept = lax.dynamic_index_in_dim(split, lane_core, 2, keepdims=False)
    chip = kept + swap(sent, "narrow", 4, 1).astype(F32)
    away = lax.dynamic_index_in_dim(chip, 1 - lane_x, 1, keepdims=False).astype(BF16)
    home = lax.dynamic_index_in_dim(chip, lane_x, 1, keepdims=False)
    return home + swap(away, "narrow", 4, 2).astype(F32)


def small_sum_narrow(value):
    value = value + swap(value, "narrow", 4, 1)
    return value + swap(value, "narrow", 4, 2)


def norm_stats(values):
    center = values - jnp.mean(values, axis=-1, keepdims=True)
    inverse = lax.rsqrt(jnp.mean(center * center, axis=-1, keepdims=True) + EPSILON)
    return center * inverse, inverse


def on_device(
    wide_count,
    tokens,
    cotangent,
    lengths,
    routes,
    qkv_weight,
    out_weight,
    up_weight,
    down_weight,
    first_gain,
    first_bias,
    second_gain,
    second_bias,
    router_weight,
):
    micro_count = tokens.shape[0]
    seq_count = micro_count * lengths.shape[1]
    slot_count = routes.shape[2]
    local_width = tokens.shape[2]
    seq_len = tokens.shape[1] // lengths.shape[1]
    row_count = seq_count * slot_count
    local_heads = local_width // HEAD_DIM
    block = qkv_weight.shape[0]
    width = block * wide_count
    wide_index = lax.axis_index("wide")
    narrow_index = lax.axis_index("narrow")
    lane_x, lane_core = narrow_index >> 1, narrow_index & 1
    column_start = narrow_index * local_width
    score_scale = HEAD_DIM ** (-0.5)

    vectors = jnp.concatenate(
        [first_gain, first_bias, second_gain, second_bias, router_weight]
    )
    first_width = qkv_weight.shape[1] * qkv_weight.shape[2] + out_weight.shape[1]
    extra = jnp.pad(vectors[None], ((0, 15), (0, first_width - vectors.shape[0])))
    first_block = jnp.concatenate(
        [jnp.concatenate([qkv_weight.reshape(block, -1), out_weight], axis=1), extra], axis=0
    )
    first_full = gather_wide(first_block, wide_index, wide_count)
    full_up = gather_wide(up_weight, wide_index, wide_count).reshape(width, -1)
    full_down = gather_wide(down_weight, wide_index, wide_count).reshape(width, -1)
    merged = first_full[:, :block].reshape(width, first_width)
    full_qkv = merged[:, : first_width - out_weight.shape[1]]
    full_out = merged[:, first_width - out_weight.shape[1] :]
    vector_rows = (
        first_full[:, block, : 5 * block]
        .reshape(wide_count, 5, block)
        .transpose(1, 0, 2)
        .reshape(5, width)
        .astype(F32)
    )
    gain_one, bias_one, gain_two, bias_two, router = [vector_rows[i] for i in range(5)]

    positions = jnp.arange(seq_len, dtype=jnp.int32)
    flat_routes = routes.reshape(seq_count, slot_count)
    live = jnp.arange(slot_count, dtype=jnp.int32)[None] < (lengths.reshape(seq_count) // 8)[:, None]
    target = jnp.where(live, flat_routes, -1)
    indicator = (target[:, :, None] == positions[None, None, :]).astype(BF16)
    token_rows = tokens.reshape(seq_count, seq_len, local_width)
    cot_rows = cotangent.reshape(seq_count, seq_len, local_width)
    picked = jnp.einsum("emp,epf->emf", indicator, token_rows, preferred_element_type=F32)
    picked = picked.astype(BF16).reshape(row_count, local_width)
    picked_cot = jnp.einsum("emp,epf->emf", indicator, cot_rows, preferred_element_type=F32)
    picked_cot = picked_cot.astype(BF16).reshape(row_count, local_width)
    chosen_low = gather_narrow(picked, lane_x, lane_core)
    cot_low = gather_narrow(picked_cot, lane_x, lane_core)
    chosen = chosen_low.astype(F32)

    gate = jnp.sum(chosen * router, axis=-1, keepdims=True)
    first_scaled, first_inverse = norm_stats(chosen)
    normed = (first_scaled * gain_one + bias_one).astype(BF16)
    qkv = jnp.dot(normed, full_qkv, preferred_element_type=F32).astype(BF16)
    split_qkv = qkv.reshape(seq_count, slot_count, 3, local_heads, HEAD_DIM)
    query, key, value = [split_qkv[:, :, i] for i in range(3)]
    causal = jnp.arange(slot_count)[:, None] >= jnp.arange(slot_count)[None, :]
    scores = jnp.einsum("sqhd,skhd->shqk", query, key, preferred_element_type=F32) * score_scale
    scores = jnp.where(causal, scores, -1e30)
    row_max = jnp.max(scores, axis=-1, keepdims=True)
    weights = jnp.exp(scores - row_max)
    probs = weights / jnp.sum(weights, axis=-1, keepdims=True)
    probs_low = probs.astype(BF16)
    heads_out = jnp.einsum("shqk,skhd->sqhd", probs_low, value, preferred_element_type=F32)
    heads_out = heads_out.reshape(row_count, local_width).astype(BF16)
    attended_low = sum_narrow(contract_last(heads_out, full_out), lane_core)
    attended = attended_low.astype(F32)
    second_scaled, second_inverse = norm_stats(chosen + attended)
    normed_two = (second_scaled * gain_two + bias_two).astype(BF16)
    hidden = jnp.dot(normed_two, full_up, preferred_element_type=F32)
    activated, gelu_pull = jax.vjp(lambda v: jax.nn.gelu(v, approximate=True), hidden)
    activated = activated.astype(BF16)

    cot = cot_low.astype(F32)
    grad_branch = gate * cot
    grad_expanded = grad_branch.astype(BF16)
    down_grad = weight_grad(grad_expanded, activated, wide_index, wide_count)
    grad_act = jnp.dot(grad_expanded, full_down, preferred_element_type=F32)
    grad_pre = gelu_pull(grad_act)[0].astype(BF16)
    grad_normed_two = sum_narrow(contract_last(grad_pre, full_up), lane_core).astype(F32)
    up_grad = weight_grad(normed_two, grad_pre, wide_index, wide_count)

    expanded_part = contract_last(activated, full_down)
    gate_part = jnp.sum((expanded_part + 0.25 * attended) * cot, axis=-1)
    own = lambda v: lax.dynamic_slice_in_dim(v, column_start, local_width, 1)
    branch = own(attended) + scatter_narrow(expanded_part, lane_x, lane_core)
    update = (gate * branch).astype(BF16).reshape(seq_count, slot_count, local_width)
    mixed = token_rows.astype(F32) + jnp.einsum(
        "yti,yto->yio", indicator, update, preferred_element_type=F32
    )
    mixed = mixed.astype(BF16).reshape(tokens.shape)

    scaled_grad = grad_normed_two * gain_two
    grad_second = second_inverse * (
        scaled_grad
        - jnp.mean(scaled_grad, axis=-1, keepdims=True)
        - second_scaled * jnp.mean(scaled_grad * second_scaled, axis=-1, keepdims=True)
    )
    second_gain_part = 0.25 * jnp.sum(grad_normed_two * second_scaled, 0)
    second_bias_part = 0.25 * jnp.sum(grad_normed_two, 0)
    grad_attended = (grad_branch + grad_second).astype(BF16)
    grad_heads = jnp.dot(grad_attended, full_out, preferred_element_type=F32).astype(BF16)
    grad_heads = grad_heads.reshape(seq_count, slot_count, local_heads, HEAD_DIM)
    grad_probs = jnp.einsum("sqhd,skhd->shqk", grad_heads, value, preferred_element_type=F32)
    row_dot = jnp.sum(probs * grad_probs, axis=-1, keepdims=True)
    grad_scores = (probs * (grad_probs - row_dot)).astype(BF16)
    grad_query = score_scale * jnp.einsum(
        "shqk,skhd->sqhd", grad_scores, key, preferred_element_type=F32
    )
    grad_key = score_scale * jnp.einsum(
        "shqk,sqhd->skhd", grad_scores, query, preferred_element_type=F32
    )
    grad_value = jnp.einsum("shqk,sqhd->skhd", probs_low, grad_heads, preferred_element_type=F32)
    grad_qkv = (
        jnp.stack([grad_query, grad_key, grad_value], axis=2)
        .reshape(row_count, 3 * local_width)
        .astype(BF16)
    )
    out_grad = weight_grad(grad_attended, heads_out, wide_index, wide_count)
    qkv_grad = weight_grad(normed, grad_qkv, wide_index, wide_count)
    normed_part = contract_last(grad_qkv, full_qkv)

    scaled_part = normed_part * gain_one
    rows_part = jnp.stack(
        [gate_part, jnp.mean(scaled_part, axis=-1), jnp.mean(scaled_part * first_scaled, axis=-1)]
    )
    first_gain_part = jnp.sum(normed_part * first_scaled, 0)
    first_bias_part = jnp.sum(normed_part, 0)
    router_part = jnp.sum(chosen * gate_part[:, None], 0)
    row_sums = small_sum_narrow(rows_part)
    grad_gate, mean_one, mean_two = [row_sums[i][:, None] for i in range(3)]
    own_row = lambda v: lax.dynamic_slice_in_dim(v, column_start, local_width, 0)
    grad_normed = scatter_narrow(normed_part, lane_x, lane_core)
    grad_first = first_inverse * (
        grad_normed * own_row(gain_one) - mean_one - own(first_scaled) * mean_two
    )
    grad_chosen = own(grad_second) + grad_first + grad_gate * own_row(router)
    update_grad = grad_chosen.astype(BF16).reshape(seq_count, slot_count, local_width)
    tokens_grad = cot_rows.astype(F32) + jnp.einsum(
        "yti,yto->yio", indicator, update_grad, preferred_element_type=F32
    )
    tokens_grad = tokens_grad.astype(BF16).reshape(cotangent.shape)

    parts = jnp.stack(
        [first_gain_part, first_bias_part, second_gain_part, second_bias_part, router_part]
    )
    parts = small_sum_narrow(parts)
    split = parts.reshape(5, wide_count // 2, 2, block)
    low = wide_index & 1
    pick = lambda which: lax.dynamic_index_in_dim(split, which, 2, keepdims=False).transpose(1, 0, 2)
    kept = pick(low) + swap(pick(1 - low), "wide", wide_count, 1)
    vector_grads = scatter_vectors(kept, wide_index, wide_count)
    return (
        mixed,
        tokens_grad,
        qkv_grad.reshape(qkv_weight.shape),
        out_grad,
        up_grad,
        down_grad,
        vector_grads[0],
        vector_grads[1],
        vector_grads[2],
        vector_grads[3],
        vector_grads[4],
    )


def scatter_vectors(kept, index, count):
    for low, width in reversed(bit_groups(count)[:-1]):
        group = 1 << width
        digit = (index >> low) & (group - 1)
        parts = kept.reshape((-1, group) + kept.shape[1:])
        take = lambda s: lax.dynamic_index_in_dim(parts, digit ^ s, 1, keepdims=False)
        received = [swap(take(s), "wide", count, s << low) for s in range(1, group)]
        kept = take(0)
        for piece in received:
            kept = kept + piece
    return kept[0]


def solution(mesh):
    wide_count = mesh.shape["wide"]

    def body(*arguments):
        return on_device(wide_count, *arguments)

    return jax.shard_map(
        body,
        mesh=mesh,
        in_specs=(
            P(None, "wide", "narrow"),
            P(None, "wide", "narrow"),
            P(None, "wide"),
            P(None, "wide", None),
            P("wide", None, "narrow"),
            P("wide", "narrow"),
            P("wide", "narrow"),
            P("wide", "narrow"),
            P("wide"),
            P("wide"),
            P("wide"),
            P("wide"),
            P("wide"),
        ),
        out_specs=(
            P(None, "wide", "narrow"),
            P(None, "wide", "narrow"),
            P("wide", None, "narrow"),
            P("wide", "narrow"),
            P("wide", "narrow"),
            P("wide", "narrow"),
            P("wide"),
            P("wide"),
            P("wide"),
            P("wide"),
            P("wide"),
        ),
        check_vma=False,
    )
```

```python
import functools

import jax
import jax.numpy as jnp
from jax import lax
from jax.experimental import pallas as pl
from jax.experimental.pallas import tpu as pltpu
from jax.sharding import PartitionSpec as P

HEAD_DIM = 64
EPSILON = 1e-05
SQRT_2_OVER_PI = 0.7978845608028654
CUBIC = 0.044715


F32 = jnp.float32
BF16 = jnp.bfloat16


def swap(value, axis, count, mask):
    return lax.ppermute(value, axis, [(i, i ^ mask) for i in range(count)])


def gather_low(block, index, count, low_bits):
    held = block[None]
    for bit in reversed(range(low_bits)):
        other = swap(held, "wide", count, 1 << bit)
        flip = ((index >> bit) & 1) != 0
        pair = [jnp.where(flip, other, held), jnp.where(flip, held, other)]
        held = jnp.stack(pair, axis=1).reshape((-1,) + block.shape)
    return held


def scatter_low(total, index, count, low_bits):
    for bit in range(low_bits):
        split = total.reshape((-1, 2) + total.shape[1:])
        digit = (index >> bit) & 1
        sent = lax.dynamic_index_in_dim(split, 1 - digit, 1, keepdims=False)
        kept = lax.dynamic_index_in_dim(split, digit, 1, keepdims=False)
        total = kept + swap(sent, "wide", count, 1 << bit)
    return total[0]


def gather_high(block, count, low_bits):
    pieces = [None] * 8
    pieces[0] = block
    for s in (2, 4, 6):
        pieces[s] = swap(block, "wide", count, s << low_bits)
    for s in (0, 2, 4, 6):
        pieces[s ^ 1] = swap(pieces[s], "wide", count, 1 << low_bits)
    return pieces


def call(body, grid, ins, outs, scratch=(), flops=0, moved=0, name=None):
    in_specs, arrays = [], []
    for array, block, index_map in ins:
        arrays.append(array)
        if block == "smem":
            in_specs.append(pl.BlockSpec(memory_space=pltpu.SMEM))
        elif block is None:
            zeros = (0,) * array.ndim
            in_specs.append(pl.BlockSpec(array.shape, lambda i, z=zeros: z))
        else:
            in_specs.append(pl.BlockSpec(block, index_map))
    out_specs = [pl.BlockSpec(block, index_map) for _, _, block, index_map in outs]
    out_shape = [jax.ShapeDtypeStruct(shape, dtype) for shape, dtype, _, _ in outs]
    return pl.pallas_call(
        body,
        grid=(grid,),
        in_specs=in_specs,
        out_specs=out_specs,
        out_shape=out_shape,
        scratch_shapes=list(scratch),
        cost_estimate=pl.CostEstimate(flops=flops, bytes_accessed=moved, transcendentals=0),
        compiler_params=pltpu.CompilerParams(dimension_semantics=("arbitrary",)),
        name=name,
    )(*arrays)


def dot(left, right):
    return jnp.dot(left, right, preferred_element_type=F32)


def dot_last(left, right):
    return lax.dot_general(left, right, (((1,), (1,)), ((), ())), preferred_element_type=F32)


def dot_first(left, right):
    return lax.dot_general(left, right, (((0,), (0,)), ((), ())), preferred_element_type=F32)


def aligned(index, size):
    return pl.ds(pl.multiple_of(index * size, size), size)


def place_rows(high, pieces, target, first, width, rows):
    for s, piece in enumerate(pieces):
        target[aligned(high ^ s, rows), :] = piece[:rows, first : first + width]


def place_columns(lane, pieces, target):
    width = pieces[0].shape[1]
    for s, piece in enumerate(pieces):
        target[:, aligned(lane ^ s, width)] = piece[...]


def split_columns(high, source, sent, kept, width):
    for s in range(4):
        here = high ^ (2 * s)
        kept[:, s * width : (s + 1) * width] = source[:, aligned(here, width)].astype(kept.dtype)
        sent[:, s * width : (s + 1) * width] = source[:, aligned(here ^ 1, width)].astype(sent.dtype)


def norm_stats(values):
    mean = jnp.mean(values, axis=-1, keepdims=True)
    center = values - mean
    inverse = lax.rsqrt(jnp.mean(center * center, axis=-1, keepdims=True) + EPSILON)
    return center * inverse, inverse, mean


def attention_probs(query, key):
    scores = dot_last(query, key) * (HEAD_DIM ** (-0.5))
    rows = lax.broadcasted_iota(jnp.int32, scores.shape, 0)
    columns = lax.broadcasted_iota(jnp.int32, scores.shape, 1)
    scores = jnp.where(rows >= columns, scores, -1e30)
    top = jnp.max(scores, axis=-1, keepdims=True)
    weights = jnp.exp(scores - top)
    return weights / jnp.sum(weights, axis=-1, keepdims=True)


def select_kernel(target_ref, source_ref, out_ref):
    slots = target_ref.shape[2]
    length = source_ref.shape[1]
    column = jnp.transpose(jnp.broadcast_to(target_ref[0], (8, slots)))[:, :1]
    positions = lax.broadcasted_iota(jnp.int32, (slots, length), 1)
    indicator = (positions == column).astype(BF16)
    out_ref[...] = dot(indicator, source_ref[0]).astype(BF16)


def forward_kernel(where, *refs, rows, width):
    pieces, picks = refs[:8], refs[8:12]
    (chosen_out, normed_sent, normed_kept, qkv_out, heads_out, sent_out, kept_out, vectors_out) = refs[12:20]
    qkv_w, out_w, scratch = refs[20:]
    high, lane, core = where[0], where[1], where[2]
    local = picks[0].shape[1]

    @pl.when(pl.program_id(0) == 0)
    def _():
        place_rows(high, pieces, qkv_w, 0, 3 * local, rows)
        place_rows(high, pieces, out_w, 3 * local, local, rows)
        vectors_out[...] = jnp.zeros_like(vectors_out)
        for s, piece in enumerate(pieces):
            row = piece[rows : rows + 1, :].astype(F32)
            for k in range(5):
                vectors_out[k : k + 1, aligned(high ^ s, rows)] = row[:, k * rows : (k + 1) * rows]

    place_columns(lane, picks, chosen_out)
    chosen = chosen_out[...].astype(F32)
    scaled, _, _ = norm_stats(chosen)
    normed = (scaled * vectors_out[0:1, :] + vectors_out[1:2, :]).astype(BF16)
    scratch[...] = normed
    split_columns(high, scratch, normed_sent, normed_kept, rows)
    qkv_out[...] = dot(normed, qkv_w[...]).astype(BF16)
    for h in range(local // HEAD_DIM):
        part = lambda k: qkv_out[:, k * local + h * HEAD_DIM : k * local + (h + 1) * HEAD_DIM]
        probs = attention_probs(part(0), part(1))
        heads_out[:, h * HEAD_DIM : (h + 1) * HEAD_DIM] = dot(probs.astype(BF16), part(2)).astype(BF16)
    half = width // 2
    heads = heads_out[...]
    sent_out[...] = dot_last(heads, out_w[aligned(1 - core, half), :]).astype(BF16)
    kept_out[...] = dot_last(heads, out_w[aligned(core, half), :])


def join_halves(core, own, other, target):
    half = own.shape[1]
    target[:, aligned(core, half)] = own[...]
    target[:, aligned(1 - core, half)] = other[...]


def middle_kernel(where, *refs, rows, width):
    ups, downs = refs[:8], refs[8:16]
    vectors, chosen_in, own, other = refs[16:20]
    picks = refs[20:24]
    (cot_out, attended_out, act_out, pre_out, two_sent, two_kept, grad_sent, grad_kept, sent_out, kept_out) = refs[24:34]
    up_w, down_w, scratch = refs[34:]
    high, lane, core = where[0], where[1], where[2]

    @pl.when(pl.program_id(0) == 0)
    def _():
        place_rows(high, ups, up_w, 0, up_w.shape[1], rows)
        place_rows(high, downs, down_w, 0, down_w.shape[1], rows)

    join_halves(core, own, other, attended_out)
    place_columns(lane, picks, cot_out)
    chosen = chosen_in[...].astype(F32)
    gate = jnp.sum(chosen * vectors[4:5, :], axis=-1, keepdims=True)
    scaled, _, _ = norm_stats(chosen + attended_out[...].astype(F32))
    normed = (scaled * vectors[2:3, :] + vectors[3:4, :]).astype(BF16)
    scratch[...] = normed
    split_columns(high, scratch, two_sent, two_kept, rows)
    grad_expanded = (gate * cot_out[...].astype(F32)).astype(BF16)
    scratch[...] = grad_expanded
    split_columns(high, scratch, grad_sent, grad_kept, rows)
    hidden = dot(normed, up_w[...])
    square = hidden * hidden
    curve = jnp.tanh(SQRT_2_OVER_PI * (hidden + CUBIC * (square * hidden)))
    act_out[...] = (0.5 * hidden * (1.0 + curve)).astype(BF16)
    slope = 0.5 * (1.0 + curve) + 0.5 * hidden * (1.0 - curve * curve) * (
        SQRT_2_OVER_PI * (1.0 + 3.0 * CUBIC * square)
    )
    grad_pre = (dot(grad_expanded, down_w[...]) * slope).astype(BF16)
    pre_out[...] = grad_pre
    half = width // 2
    sent_out[...] = dot_last(grad_pre, up_w[aligned(1 - core, half), :]).astype(BF16)
    kept_out[...] = dot_last(grad_pre, up_w[aligned(core, half), :])


def expand_kernel(where, *refs, rows, width):
    downs = refs[:8]
    act, attended, cot = refs[8:11]
    sent_out, kept_out, gate_out = refs[11:14]
    (down_w,) = refs[14:]
    high, lane = where[0], where[1]

    @pl.when(pl.program_id(0) == 0)
    def _():
        place_rows(high, downs, down_w, 0, down_w.shape[1], rows)

    local = width // 4
    gate_part = 0.25 * jnp.sum(attended[...].astype(F32) * cot[...].astype(F32), axis=-1, keepdims=True)
    for entry, (flip, target) in enumerate(((3, sent_out), (1, sent_out), (2, kept_out), (0, kept_out))):
        chunk = aligned(lane ^ flip, local)
        value = dot_last(act[...], down_w[chunk, :])
        gate_part = gate_part + jnp.sum(value * cot[:, chunk].astype(F32), axis=-1, keepdims=True)
        target[entry % 2] = value.astype(target.dtype)
    gate_out[...] = jnp.broadcast_to(gate_part, gate_out.shape)


def backward_kernel(where, *refs, rows, width):
    pieces = refs[:8]
    vectors, chosen_in, attended, cot, qkv, grad_own, grad_other, gate_in = refs[8:16]
    (att_sent, att_kept, grad_qkv, second_own, sent_out, kept_out, stats_out, sums_sent, sums_kept, local_out) = refs[16:26]
    qkv_w, out_w, scratch, low_scratch, sums = refs[26:]
    high, lane, core = where[0], where[1], where[2]
    step = pl.program_id(0)
    local = qkv.shape[1] // 3

    @pl.when(step == 0)
    def _():
        place_rows(high, pieces, qkv_w, 0, 3 * local, rows)
        place_rows(high, pieces, out_w, 3 * local, local, rows)
        sums[...] = jnp.zeros_like(sums)

    join_halves(core, grad_own, grad_other, low_scratch)
    chosen = chosen_in[...].astype(F32)
    gate = jnp.sum(chosen * vectors[4:5, :], axis=-1, keepdims=True)
    scaled, inverse, _ = norm_stats(chosen + attended[...].astype(F32))
    grad_two = low_scratch[...].astype(F32)
    sums[2:3, :] += 0.25 * jnp.sum(grad_two * scaled, axis=0, keepdims=True)
    sums[3:4, :] += 0.25 * jnp.sum(grad_two, axis=0, keepdims=True)
    pulled = grad_two * vectors[2:3, :]
    grad_second = inverse * (
        pulled
        - jnp.mean(pulled, axis=-1, keepdims=True)
        - scaled * jnp.mean(pulled * scaled, axis=-1, keepdims=True)
    )
    scratch[...] = grad_second
    second_own[...] = scratch[:, aligned(lane, local)]
    grad_attended = (gate * cot[...].astype(F32) + grad_second).astype(BF16)
    low_scratch[...] = grad_attended
    split_columns(high, low_scratch, att_sent, att_kept, rows)
    grad_heads = dot(grad_attended, out_w[...]).astype(BF16)
    scale = HEAD_DIM ** (-0.5)
    for h in range(local // HEAD_DIM):
        columns = lambda k: slice(k * local + h * HEAD_DIM, k * local + (h + 1) * HEAD_DIM)
        query, key, value = [qkv[:, columns(k)] for k in range(3)]
        grad_out = grad_heads[:, h * HEAD_DIM : (h + 1) * HEAD_DIM]
        probs = attention_probs(query, key)
        grad_probs = dot_last(grad_out, value)
        row_dot = jnp.sum(probs * grad_probs, axis=-1, keepdims=True)
        grad_scores = (probs * (grad_probs - row_dot)).astype(BF16)
        grad_qkv[:, columns(0)] = (scale * dot(grad_scores, key)).astype(BF16)
        grad_qkv[:, columns(1)] = (scale * dot_first(grad_scores, query)).astype(BF16)
        grad_qkv[:, columns(2)] = dot_first(probs.astype(BF16), grad_out).astype(BF16)
    first_scaled, first_inverse, first_mean = norm_stats(chosen)
    scratch[...] = first_scaled
    mean_one = jnp.zeros_like(gate)
    mean_two = jnp.zeros_like(gate)
    for entry, (flip, target) in enumerate(((3, sent_out), (1, sent_out), (2, kept_out), (0, kept_out))):
        chunk = aligned(lane ^ flip, local)
        value = dot_last(grad_qkv[...], qkv_w[chunk, :])
        target[entry % 2] = value.astype(target.dtype)
        normal = scratch[:, chunk]
        weighted = value * normal
        sums[0:1, chunk] += jnp.sum(weighted, axis=0, keepdims=True)
        sums[1:2, chunk] += jnp.sum(value, axis=0, keepdims=True)
        gain = vectors[0:1, chunk]
        mean_one = mean_one + jnp.sum(value * gain, axis=-1, keepdims=True)
        mean_two = mean_two + jnp.sum(weighted * gain, axis=-1, keepdims=True)
    gate_part = gate_in[:, :1]
    sums[4:5, :] += jnp.sum(chosen * gate_part, axis=0, keepdims=True)
    lanes = lax.broadcasted_iota(jnp.int32, gate_in.shape, 1)
    table = jnp.where(
        lanes == 0,
        gate_in[...],
        jnp.where(lanes == 1, mean_one / width, jnp.where(lanes == 2, mean_two / width, 0.0)),
    )
    stats_out[...] = jnp.transpose(table)[:8]
    local_out[...] = jnp.where(lanes == 0, first_inverse, jnp.where(lanes == 1, first_mean, 0.0))

    @pl.when(step == pl.num_programs(0) - 1)
    def _():
        split_columns(high, sums, sums_sent, sums_kept, rows)


def scatter_rows(target_ref, base, update, out_ref):
    length, slots = base.shape[1], target_ref.shape[2]
    positions = lax.broadcasted_iota(jnp.int32, (length, slots), 0)
    indicator = (positions == target_ref[0]).astype(BF16)
    out_ref[0] = (base[0].astype(F32) + dot(indicator, update)).astype(BF16)


def mixed_kernel(where, target, tokens, vectors, chosen, attended, home, received, out_ref):
    lane = where[1]
    local = home.shape[1]
    gate = jnp.sum(chosen[...].astype(F32) * vectors[4:5, :], axis=-1, keepdims=True)
    branch = attended[:, aligned(lane, local)].astype(F32) + home[...] + received[...].astype(F32)
    scatter_rows(target, tokens, (gate * branch).astype(BF16), out_ref)


def input_grad_kernel(where, target, cot, vectors, picked, second, home, received, stats, local_in, out_ref):
    lane = where[1]
    local = home.shape[1]
    chunk = aligned(lane, local)
    columns = jnp.transpose(stats[...])
    grad_gate, mean_one, mean_two = [columns[:, k : k + 1] for k in range(3)]
    inverse, mean = local_in[:, 0:1], local_in[:, 1:2]
    grad_normed = home[...] + received[...].astype(F32)
    scaled = (picked[...].astype(F32) - mean) * inverse
    grad_first = inverse * (grad_normed * vectors[0:1, chunk] - mean_one - scaled * mean_two)
    update = second[...] + grad_first + grad_gate * vectors[4:5, chunk]
    scatter_rows(target, cot, update.astype(BF16), out_ref)


def on_device(
    wide_count,
    tokens,
    cotangent,
    lengths,
    routes,
    qkv_weight,
    out_weight,
    up_weight,
    down_weight,
    first_gain,
    first_bias,
    second_gain,
    second_bias,
    router_weight,
):
    seqs = tokens.shape[0] * lengths.shape[1]
    slots = routes.shape[2]
    local = tokens.shape[2]
    seq_len = tokens.shape[1] // lengths.shape[1]
    total_rows = seqs * slots
    low_bits = wide_count.bit_length() - 4
    low_count = 1 << low_bits
    block = qkv_weight.shape[0]
    rows = block * low_count
    width = rows * 8
    hidden = up_weight.shape[1]
    wide_index = lax.axis_index("wide")
    lane = lax.axis_index("narrow")
    high = wide_index >> low_bits
    where = jnp.stack([high, lane, lane & 1]).astype(jnp.int32)

    merged = jnp.concatenate([qkv_weight.reshape(block, -1), out_weight], axis=1)
    vectors = jnp.stack([first_gain, first_bias, second_gain, second_bias, router_weight])
    if low_bits:
        low = lambda v: gather_low(v, wide_index, wide_count, low_bits)
        merged = low(merged).reshape(rows, -1)
        up_weight = low(up_weight).reshape(rows, -1)
        down_weight = low(down_weight).reshape(rows, -1)
        vectors = low(vectors).transpose(1, 0, 2).reshape(5, rows)
    extra = jnp.pad(vectors.reshape(1, -1), ((0, 15), (0, merged.shape[1] - 5 * rows)))
    first_pieces = gather_high(jnp.concatenate([merged, extra], axis=0), wide_count, low_bits)
    up_pieces = gather_high(up_weight, wide_count, low_bits)
    down_pieces = gather_high(down_weight, wide_count, low_bits)

    live = jnp.arange(slots, dtype=jnp.int32)[None] < (lengths.reshape(seqs) // 8)[:, None]
    target = jnp.where(live, routes.reshape(seqs, slots), -1)[:, None, :]
    token_rows = tokens.reshape(seqs, seq_len, local)
    cot_rows = cotangent.reshape(seqs, seq_len, local)
    by_seq = lambda i: (i, 0, 0)
    by_row = lambda i: (i, 0)
    pair = lambda i: (0, i, 0)
    fixed = lambda i: (0, 0)
    target_in = (target, (1, 1, slots), by_seq)
    rows_in = lambda v: (v, (slots, v.shape[1]), by_row)
    rows_out = lambda columns, dtype: ((total_rows, columns), dtype, (slots, columns), by_row)
    pair_out = lambda dtype: ((2, total_rows, local), dtype, (2, slots, local), pair)
    whole = lambda v: (v, None, None)
    info = (where, "smem", None)
    spread = dict(rows=rows, width=width)

    def select(source, name):
        return call(
            select_kernel,
            seqs,
            [target_in, (source, (1, seq_len, local), by_seq)],
            [rows_out(local, BF16)],
            flops=2 * total_rows * seq_len * local,
            moved=2 * source.size,
            name=name,
        )[0]

    def gather_narrow(own):
        across = swap(own, "narrow", 4, 2)
        return [own, swap(own, "narrow", 4, 1), across, swap(across, "narrow", 4, 1)]

    def finish_sum(sent, kept):
        chip = (kept + swap(sent, "narrow", 4, 1).astype(F32)).astype(BF16)
        total = chip + swap(chip, "narrow", 4, 2)
        return total, swap(total, "narrow", 4, 1)

    def finish_scatter(sent, kept):
        received = swap(sent, "narrow", 4, 1)
        away = (kept[0] + received[0].astype(F32)).astype(BF16)
        return kept[1] + received[1].astype(F32), swap(away, "narrow", 4, 2)

    picked = select(token_rows, "select_tokens")
    picks = gather_narrow(picked)
    picked_cot = select(cot_rows, "select_cot")
    cot_picks = gather_narrow(picked_cot)

    (chosen, normed_sent, normed_kept, qkv, heads, sent, kept, table) = call(
        functools.partial(forward_kernel, **spread),
        seqs,
        [info] + [whole(p) for p in first_pieces] + [rows_in(p) for p in picks],
        [
            rows_out(width, BF16),
            rows_out(width // 2, BF16),
            rows_out(width // 2, BF16),
            rows_out(3 * local, BF16),
            rows_out(local, BF16),
            rows_out(width // 2, BF16),
            rows_out(width // 2, F32),
            ((8, width), F32, (8, width), fixed),
        ],
        scratch=[
            pltpu.VMEM((width, 3 * local), BF16),
            pltpu.VMEM((width, local), BF16),
            pltpu.VMEM((slots, width), BF16),
        ],
        flops=2 * total_rows * width * 4 * local,
        moved=20 << 20,
        name="forward",
    )
    attended_own, attended_other = finish_sum(sent, kept)

    (cot, attended, activated, grad_pre, two_sent, two_kept, grad_sent, grad_kept, sent, kept) = call(
        functools.partial(middle_kernel, **spread),
        seqs,
        [info]
        + [whole(p) for p in up_pieces]
        + [whole(p) for p in down_pieces]
        + [whole(table), rows_in(chosen), rows_in(attended_own), rows_in(attended_other)]
        + [rows_in(p) for p in cot_picks],
        [
            rows_out(width, BF16),
            rows_out(width, BF16),
            rows_out(hidden, BF16),
            rows_out(hidden, BF16),
            rows_out(width // 2, BF16),
            rows_out(width // 2, BF16),
            rows_out(width // 2, BF16),
            rows_out(width // 2, BF16),
            rows_out(width // 2, BF16),
            rows_out(width // 2, F32),
        ],
        scratch=[
            pltpu.VMEM((width, hidden), BF16),
            pltpu.VMEM((width, hidden), BF16),
            pltpu.VMEM((slots, width), BF16),
        ],
        flops=6 * total_rows * width * hidden,
        moved=30 << 20,
        name="middle",
    )
    grad_own, grad_other = finish_sum(sent, kept)

    def weight_grad(left_sent, left_kept, right):
        sent_part = dot_first(left_sent, right).astype(BF16)
        received = swap(sent_part, "wide", wide_count, 1 << low_bits)
        side = dot_first(left_kept, right) + received.astype(F32)
        away = [
            swap(side[s * rows : (s + 1) * rows].astype(BF16), "wide", wide_count, (2 * s) << low_bits)
            for s in range(1, 4)
        ]
        total = side[:rows]
        for piece in away:
            total = total + piece.astype(F32)
        if low_bits:
            total = scatter_low(total.reshape(low_count, block, -1), wide_index, wide_count, low_bits)
        return total

    down_grad = weight_grad(grad_sent, grad_kept, activated)
    up_grad = weight_grad(two_sent, two_kept, grad_pre)

    sent, kept, gate_part = call(
        functools.partial(expand_kernel, **spread),
        seqs,
        [info] + [whole(p) for p in down_pieces] + [rows_in(activated), rows_in(attended), rows_in(cot)],
        [pair_out(BF16), pair_out(F32), rows_out(128, F32)],
        scratch=[pltpu.VMEM((width, hidden), BF16)],
        flops=2 * total_rows * width * hidden,
        moved=16 << 20,
        name="expand",
    )
    home, received = finish_scatter(sent, kept)
    mixed = call(
        mixed_kernel,
        seqs,
        [info, target_in, (token_rows, (1, seq_len, local), by_seq), whole(table)]
        + [rows_in(v) for v in (chosen, attended, home, received)],
        [((seqs, seq_len, local), BF16, (1, seq_len, local), by_seq)],
        flops=2 * total_rows * seq_len * local,
        moved=12 << 20,
        name="mixed",
    )[0]

    (att_sent, att_kept, grad_qkv, second_own, sent, kept, stats, sums_sent, sums_kept, norm_one) = call(
        functools.partial(backward_kernel, **spread),
        seqs,
        [info]
        + [whole(p) for p in first_pieces]
        + [whole(table)]
        + [rows_in(v) for v in (chosen, attended, cot, qkv, grad_own, grad_other, gate_part)],
        [
            rows_out(width // 2, BF16),
            rows_out(width // 2, BF16),
            rows_out(3 * local, BF16),
            rows_out(local, F32),
            pair_out(BF16),
            pair_out(F32),
            ((8, total_rows), F32, (8, slots), lambda i: (0, i)),
            ((8, width // 2), F32, (8, width // 2), fixed),
            ((8, width // 2), F32, (8, width // 2), fixed),
            rows_out(128, F32),
        ],
        scratch=[
            pltpu.VMEM((width, 3 * local), BF16),
            pltpu.VMEM((width, local), BF16),
            pltpu.VMEM((slots, width), F32),
            pltpu.VMEM((slots, width), BF16),
            pltpu.VMEM((8, width), F32),
        ],
        flops=2 * total_rows * width * 4 * local,
        moved=24 << 20,
        name="backward",
    )
    qkv_grad = weight_grad(normed_sent, normed_kept, grad_qkv)
    home, received = finish_scatter(sent, kept)
    small = jnp.concatenate([stats, sums_sent, sums_kept], axis=1)
    small = small + swap(small, "narrow", 4, 1)
    small = small + swap(small, "narrow", 4, 2)
    stats = small[:, :total_rows]
    sums_sent = small[:, total_rows : total_rows + width // 2]
    sums_kept = small[:, total_rows + width // 2 :]
    out_grad = weight_grad(att_sent, att_kept, heads)
    tokens_grad = call(
        input_grad_kernel,
        seqs,
        [info, target_in, (cot_rows, (1, seq_len, local), by_seq), whole(table)]
        + [rows_in(v) for v in (picked, second_own, home, received)]
        + [(stats, (8, slots), lambda i: (0, i)), rows_in(norm_one)],
        [((seqs, seq_len, local), BF16, (1, seq_len, local), by_seq)],
        flops=2 * total_rows * seq_len * local,
        moved=12 << 20,
        name="input_grad",
    )[0]

    side = sums_kept + swap(sums_sent, "wide", wide_count, 1 << low_bits)
    sums = side[:, :rows]
    for s in range(1, 4):
        sums = sums + swap(side[:, s * rows : (s + 1) * rows], "wide", wide_count, (2 * s) << low_bits)
    if low_bits:
        split = sums.reshape(8, low_count, block).transpose(1, 0, 2)
        sums = scatter_low(split, wide_index, wide_count, low_bits)
    return (
        mixed.reshape(tokens.shape),
        tokens_grad.reshape(cotangent.shape),
        qkv_grad.reshape(qkv_weight.shape),
        out_grad,
        up_grad,
        down_grad,
        sums[0],
        sums[1],
        sums[2],
        sums[3],
        sums[4],
    )


def solution(mesh):
    wide_count = mesh.shape["wide"]

    def body(*arguments):
        return on_device(wide_count, *arguments)

    return jax.shard_map(
        body,
        mesh=mesh,
        in_specs=(
            P(None, "wide", "narrow"),
            P(None, "wide", "narrow"),
            P(None, "wide"),
            P(None, "wide", None),
            P("wide", None, "narrow"),
            P("wide", "narrow"),
            P("wide", "narrow"),
            P("wide", "narrow"),
            P("wide"),
            P("wide"),
            P("wide"),
            P("wide"),
            P("wide"),
        ),
        out_specs=(
            P(None, "wide", "narrow"),
            P(None, "wide", "narrow"),
            P("wide", None, "narrow"),
            P("wide", "narrow"),
            P("wide", "narrow"),
            P("wide", "narrow"),
            P("wide"),
            P("wide"),
            P("wide"),
            P("wide"),
            P("wide"),
        ),
        check_vma=False,
    )
```
